128 devices in a mesh: section: 2 (over z_hi), ep: 32 (over x, y, core), dp: 2 (over z_lo).
Axes of the slice: x: 4, y: 4, z: 4 (z_hi: 2, z_lo: 2; z = z_hi * 2 + z_lo), core: 2. Of those that a mesh axis runs over, the one named last changes fastest.
Arguments:
- samples: float32 [4, 128, 64, 160], P(('section', 'dp'), None, 'ep'), may hold values from -0.3 to 0.3
- req_frames: int32 [4, 32, 4], P(('section', 'dp'), 'ep'), may hold values from 1 to 64, 128 in all within a row
- w_in: bfloat16 [128, 1280], replicated, may hold values from -0.5 to 0.5
- w_up_aud: bfloat16 [1280, 2560], P(None, 'dp'), may hold values from -0.15625 to 0.15625
- w_down_aud: bfloat16 [2560, 1280], P('dp'), may hold values from -0.125 to 0.125
- w_out: bfloat16 [1280, 2048], replicated, may hold values from -0.15625 to 0.15625
- norm_gain: float32 [2048], replicated, may hold values from 0.1 to 1.9
- expert_ids: int32 [4, 4096, 8], P(('section', 'dp'), 'ep'), may hold values from 0 to 63, all different within a row; in each aligned block of 128 rows (0 to 127, 128 to 255, ..., all dimensions but the last counted through in order) at most 20 rows name the same one
- gate_weights: float32 [4, 4096, 8], P(('section', 'dp'), 'ep'), may hold values from 0.03 to 0.3
- cotangent: bfloat16 [4, 4096, 2048], P(('section', 'dp'), 'ep'), may hold values from -1.5 to 1.5
- w_gate_up: bfloat16 [64, 2048, 1536], P(('section', 'ep')), may hold values from -0.125 to 0.125
- w_down: bfloat16 [64, 768, 2048], P(('section', 'ep')), may hold values from -0.21875 to 0.21875
Outputs:
- grad_x: bfloat16 [4, 4096, 2048], P(('section', 'dp'), 'ep')
- grad_w: bfloat16 [4, 4096, 8], P(('section', 'dp'), 'ep')
The draws below stay inside these ranges and needn't reach their ends.
Inputs may be any that keep to these rules, and one draw needn't show every extreme that they name: `req_frames`: the 4 counts of each packed sequence sum to 128, and the largest of them is 64. `expert_ids`: the 8 experts of a token are distinct. Among the tokens of one packed sequence no expert is named more than 20 times, and in every draw some expert is named exactly 20 times there.
All inputs are finite; a program needn't handle non-finite values.
Results may differ from the reference program's by a relative error of at most 0.023.
Values may be sent and summed in bfloat16 or wider, within the bound.
A program may use at most 128 MiB of HBM per device.

```python
import math
import jax
import jax.numpy as jnp
import numpy as np
from jax import lax

D = 2048
HID = 768
TOP = 8
D_AUD = 1280
MEL = 128
FF_AUD = 2560
NFFT = 400
HOP = 160
TIME = 64
RQ_DEV = 4
TOK_DEV = 128
REQS = 128
PACKS = 32
TOKENS = 4096
GROUPS = 4
EXPERTS = 64
CAP = 20


def block_scale(key, dims, split, smallest, top_value):
    level, own = 1.0, jax.random.fold_in(key, 6)
    for position, shards_of in split:
        heights = jnp.exp(jax.random.uniform(jax.random.fold_in(own, position), (shards_of,), jnp.float32, smallest / len(split), top_value / len(split)))
        level = level * jnp.repeat(heights, dims[position] // shards_of).reshape([-1 if axis == position else 1 for axis in range(len(dims))])
    return level


def split_up(number_of, total, limit, lean):
    portions = [(1 << 20) // math.isqrt(grade ** lean) + 1 for grade in range(2, number_of + 1)]
    spare, holding = total - limit - (number_of - 1), [1] * (number_of - 1)
    while spare > 0:
        free = [i for i in range(number_of - 1) if holding[i] < limit]
        whole, remaining = sum([portions[i] for i in free]), spare
        for i in free:
            more = min(limit - holding[i], max(1, remaining * portions[i] // whole), spare)
            holding[i] = holding[i] + more
            spare = spare - more
    return np.array([limit] + holding)


def uneven(key, amount, total, limit, lean):
    if amount == 2:
        one = jax.random.randint(key, (), max(1, total - limit), min(limit, total - 1) + 1)
        return jnp.stack([one, total - one])
    sizes = jnp.asarray(split_up(amount, total, limit, lean), jnp.int32)
    twos = (amount - 1) // 2
    donor, taker = sizes[1:1 + 2 * twos:2], sizes[2:2 + 2 * twos:2]
    margin = jnp.minimum(donor - 1, limit - taker)
    passed = jax.random.randint(jax.random.fold_in(key, 1), (twos,), 0, 1 << 20) % (margin + 1)
    sizes = sizes.at[1:1 + 2 * twos:2].set(donor - passed).at[2:2 + 2 * twos:2].set(taker + passed)
    return sizes[jax.random.permutation(jax.random.fold_in(key, 2), amount)]


def deal_out(stream_key, own, number, rows, amount, top, most, lean):
    sequence = jax.random.permutation(stream_key, amount)
    packed, ordinary = shares(amount, rows * top, most, lean, True), shares(amount, rows * top, most, lean, False)
    places = jnp.arange(amount)

    def named(tallies, offset_by):
        used = int((tallies > 0).sum())
        fixed = max(1, used // 4)
        shifted = fixed + (places - fixed + offset_by * (used - fixed)) % max(1, amount - fixed)
        return jnp.zeros((amount,), jnp.int32).at[sequence[jnp.where(places < fixed, places, shifted)]].set(jnp.asarray(tallies, jnp.int32))

    tallies = jnp.where(number % 4 == 0, named(packed, number // 4), named(ordinary, number - number // 4 - 1))
    mixed = jax.random.permutation(jax.random.fold_in(own, 3), amount)
    giver, taker = mixed[0:amount // 2 * 2:2], mixed[1:amount // 2 * 2:2]
    margin = jnp.minimum(tallies[giver] - 1, most - tallies[taker]) // 2
    margin = jnp.where((giver == sequence[0]) | (taker == sequence[0]) | (tallies[taker] == 0), 0, jnp.maximum(margin, 0))
    shifted = jax.random.randint(jax.random.fold_in(own, 4), (amount // 2,), 0, 1 << 20) % (margin + 1)
    tallies = tallies.at[giver].add(-shifted).at[taker].add(shifted)
    members = jnp.searchsorted(jnp.cumsum(tallies), jnp.arange(rows * top), side="right").astype(jnp.int32)
    grid = members.reshape(top, rows).T
    grid = grid[jax.random.permutation(jax.random.fold_in(own, 1), rows)]
    offset_by = jax.random.randint(jax.random.fold_in(own, 2), (rows, 1), 0, top)
    return jnp.take_along_axis(grid, (jnp.arange(top)[None, :] + offset_by) % top, axis=1)


def shares(number_of, total, most, skew, full):
    portions = [(1 << 20) // math.isqrt(grade ** skew) + 1 for grade in range(1, number_of + 1)]
    largest = most if full else min(most, max(-(-total // number_of), total * portions[0] // sum(portions)))
    least = 1 if total - largest >= number_of - 1 else 0
    counts, rest = [largest] + [least] * (number_of - 1), total - largest - least * (number_of - 1)
    while rest > 0:
        free = [i for i in range(1, number_of) if counts[i] < largest] or [i for i in range(1, number_of) if counts[i] < most]
        whole, left = sum([portions[i] for i in free]), rest
        for i in free:
            more = min(most - counts[i], max(1, left * portions[i] // whole), rest)
            counts[i] = counts[i] + more
            rest = rest - more
    return np.array(counts)


def gaussian(own_key, dims, spread, bound, cuts=(), held_as=jnp.bfloat16):
    level = block_scale(own_key, dims, cuts, -0.22, 0.18) if cuts else 1.0
    drawn = jax.random.normal(own_key, dims, jnp.float32) * spread * level
    return jnp.minimum(jnp.maximum(drawn, -bound), bound).astype(held_as)


def setup_inputs(seed: int = 0) -> dict:
    seeds = jax.random.split(jax.random.key(seed), 13)
    samples = gaussian(seeds[0], (GROUPS, REQS, TIME, HOP), 0.05, 0.3, ((0, 4), (2, 32)), jnp.float32)
    req_frames = jax.vmap(lambda own: uneven(own, RQ_DEV, TOK_DEV, TIME, 1))(jax.random.split(seeds[1], GROUPS * PACKS)).reshape((GROUPS, PACKS, RQ_DEV)).astype(jnp.int32)
    w_in = gaussian(seeds[2], (MEL, D_AUD), MEL ** -0.5, 0.5)
    w_up_aud = gaussian(seeds[3], (D_AUD, FF_AUD), D_AUD ** -0.5, 0.15625, ((1, 2),))
    w_down_aud = gaussian(seeds[4], (FF_AUD, D_AUD), FF_AUD ** -0.5, 0.125, ((0, 2),))
    w_out = gaussian(seeds[5], (D_AUD, D), D_AUD ** -0.5, 0.15625)
    norm_gain = jnp.clip(1.0 + 0.18 * jax.random.normal(seeds[6], (D,), jnp.float32), 0.1, 1.9)
    expert_ids_keys = jax.random.split(jax.random.fold_in(seeds[7], 1), GROUPS * TOKENS // TOK_DEV)
    expert_ids_turns = jax.random.permutation(jax.random.fold_in(seeds[7], 3), GROUPS * TOKENS // TOK_DEV)
    expert_ids = jax.vmap(lambda own, number: deal_out(jax.random.fold_in(seeds[7], 2), own, number, TOK_DEV, EXPERTS, TOP, CAP, 1))(expert_ids_keys, expert_ids_turns).reshape((GROUPS, TOKENS, TOP))
    gate_weights = jnp.clip(jnp.exp(math.log(0.3) - 2.3025852 * jax.random.uniform(seeds[8], (GROUPS, TOKENS, TOP), jnp.float32) ** block_scale(seeds[8], (GROUPS, TOKENS, TOP), ((0, 4), (1, 32)), -0.2, 0.2)), 0.03, 0.3)
    cotangent = gaussian(seeds[9], (GROUPS, TOKENS, D), 0.25, 1.5, ((0, 4), (1, 32)))
    w_gate_up = gaussian(seeds[10], (EXPERTS, D, 2 * HID), D ** -0.5, 0.125, ((0, 64),))
    w_down = gaussian(seeds[11], (EXPERTS, HID, D), HID ** -0.5, 0.21875, ((0, 64),))
    return {"samples": samples, "req_frames": req_frames, "w_in": w_in, "w_up_aud": w_up_aud, "w_down_aud": w_down_aud, "w_out": w_out, "norm_gain": norm_gain, "expert_ids": expert_ids, "gate_weights": gate_weights, "cotangent": cotangent, "w_gate_up": w_gate_up, "w_down": w_down}


MEL_FLOOR = 0.1
EPS_LAYER = 1e-05
EPS_ROOT = 1e-06
SAMPLE_RATE = 16000.0

def mel_scale(frequency):
    frequency = np.asarray(frequency) * 1.0
    log_part = 15.0 + np.log(np.maximum(frequency, 1000.0) / 1000.0) * 27.0 / math.log(6.4)
    return np.where(frequency < 1000.0, frequency * 3.0 / 200.0, log_part)

def mel_inverse(levels):
    levels = np.asarray(levels) * 1.0
    log_part = 1000.0 * np.exp((np.maximum(levels, 15.0) - 15.0) * math.log(6.4) / 27.0)
    return np.where(levels < 15.0, levels * 200.0 / 3.0, log_part)

def mel_table(bins_count, mel_count, frame_size):
    edges = mel_inverse(np.linspace(0.0, float(mel_scale(SAMPLE_RATE / 2.0)), mel_count + 2))
    centers = (np.arange(bins_count) * 1.0)[:, None] * SAMPLE_RATE / frame_size
    lower = edges[:-2][None, :]
    middle = edges[1:-1][None, :]
    upper = edges[2:][None, :]
    rising = (centers - lower) / (middle - lower)
    falling = (upper - centers) / (upper - middle)
    return np.maximum(0.0, np.minimum(rising, falling))

def sinusoid_table(times, width):
    half = width // 2
    rates = jnp.exp(-math.log(10000.0) * jnp.arange(half, dtype=jnp.float32) / (half - 1))
    angles = times.astype(jnp.float32)[:, None] * rates[None, :]
    return jnp.concatenate([jnp.sin(angles), jnp.cos(angles)], axis=1)

def layer_norm(values):
    centered = values - lax.optimization_barrier(jnp.mean(values, axis=-1, keepdims=True))
    return centered * lax.rsqrt(lax.optimization_barrier(jnp.mean(centered * centered, axis=-1, keepdims=True)) + EPS_LAYER)

def normalize(values, gain):
    return values * lax.rsqrt(lax.optimization_barrier(jnp.mean(values * values, axis=-1, keepdims=True)) + EPS_ROOT) * gain

def pack_index(lengths, total):
    ends = jnp.cumsum(lengths, axis=-1)
    positions = jnp.arange(total, dtype=jnp.int32)
    request = lax.optimization_barrier(jnp.sum((positions[:, None] >= ends[..., None, :-1]).astype(jnp.int32), axis=-1))
    starts = ends - lengths
    offset = jnp.take_along_axis(starts, request, axis=-1)
    return (request.astype(jnp.int32), (positions - offset).astype(jnp.int32))

def rank_in_block(flat, experts):
    onehot = (flat[..., None] == jnp.arange(experts, dtype=jnp.int32)).astype(jnp.int32)
    return lax.optimization_barrier(jnp.sum((jnp.cumsum(onehot, axis=1) - 1) * onehot, axis=-1)).astype(jnp.int32)

def encode(frames, times, w_in, w_up_aud, w_down_aud, w_out):
    count = frames.shape[-1]
    window = 0.5 - 0.5 * jnp.cos(2.0 * math.pi * jnp.arange(count, dtype=jnp.float32) / count)
    spectrum = jnp.fft.rfft(frames * window, axis=-1)
    power = jnp.real(spectrum) ** 2 + jnp.imag(spectrum) ** 2
    table = jnp.asarray(mel_table(power.shape[-1], w_in.shape[0], count), dtype=jnp.float32)
    energy = jnp.dot(power, table, precision=lax.Precision.HIGHEST, preferred_element_type=jnp.float32)
    log_mel = jnp.log(jnp.maximum(energy, MEL_FLOOR)).astype(jnp.bfloat16)
    state = jnp.dot(log_mel, w_in, preferred_element_type=jnp.float32) + sinusoid_table(times, w_in.shape[1])
    normed_audio = layer_norm(state).astype(jnp.bfloat16)
    hidden_audio = jax.nn.gelu(jnp.dot(normed_audio, w_up_aud, preferred_element_type=jnp.float32), approximate=False).astype(jnp.bfloat16)
    state = state + jnp.dot(hidden_audio, w_down_aud, preferred_element_type=jnp.float32)
    final_audio = layer_norm(state).astype(jnp.bfloat16)
    return jnp.dot(final_audio, w_out, preferred_element_type=jnp.float32).astype(jnp.bfloat16)

def expert_pass(rows, grads, gate_up_weight, down_weight):
    hidden_count = down_weight.shape[0]
    both = jnp.dot(rows, gate_up_weight, preferred_element_type=jnp.float32)
    gate = both[:, :hidden_count]
    upper = both[:, hidden_count:]
    sigma = jax.nn.sigmoid(gate)
    active = (gate * sigma * upper).astype(jnp.bfloat16)
    output = jnp.dot(active, down_weight, preferred_element_type=jnp.float32).astype(jnp.bfloat16)
    back = jnp.dot(grads, down_weight.T, preferred_element_type=jnp.float32)
    d_gate = back * upper * sigma * (1.0 + gate * (1.0 - sigma))
    d_upper = back * gate * sigma
    d_both = jnp.concatenate([d_gate, d_upper], axis=1).astype(jnp.bfloat16)
    d_rows = jnp.dot(d_both, gate_up_weight.T, preferred_element_type=jnp.float32).astype(jnp.bfloat16)
    return (output, d_rows)

def reference(samples, req_frames, w_in, w_up_aud, w_down_aud, w_out, norm_gain, expert_ids, gate_weights, cotangent, w_gate_up, w_down):
    hop = samples.shape[-1]
    extra = (NFFT + hop - 1) // hop - 1

    def encode_group(inputs):
        group_samples, group_lengths = inputs
        padded = jnp.concatenate([group_samples, jnp.zeros((REQS, extra, hop), jnp.float32)], axis=1)
        request, times = pack_index(group_lengths, TOK_DEV)
        owner = request + RQ_DEV * jnp.arange(PACKS, dtype=jnp.int32)[:, None]
        parts = [padded[owner, times + offset] for offset in range(extra + 1)]
        frames = jnp.concatenate(parts, axis=-1)[..., :NFFT].reshape(PACKS * TOK_DEV, NFFT)
        return encode(frames, times.reshape(-1), w_in, w_up_aud, w_down_aud, w_out)
    features = lax.map(encode_group, (samples, req_frames)).reshape(GROUPS * TOKENS, D)
    total_rows = GROUPS * TOKENS
    values = features.astype(jnp.float32)
    normed = normalize(values, norm_gain).astype(jnp.bfloat16)
    grads = cotangent.reshape(total_rows, D)
    weights = jnp.concatenate([gate_weights.reshape(total_rows * TOP), jnp.zeros((1,), jnp.float32)])
    chosen = expert_ids.reshape(total_rows // TOK_DEV, TOK_DEV * TOP)
    rank = rank_in_block(chosen, EXPERTS).reshape(-1)
    assignment = jnp.arange(total_rows * TOP, dtype=jnp.int32)
    block = assignment // (TOK_DEV * TOP)
    slot_count = total_rows // TOK_DEV * CAP
    table = jnp.full((EXPERTS, slot_count), total_rows * TOP, jnp.int32)
    table = table.at[chosen.reshape(-1), block * CAP + rank].set(assignment)
    pad_rows = jnp.concatenate([normed, jnp.zeros((1, D), jnp.bfloat16)])
    pad_grads = jnp.concatenate([grads, jnp.zeros((1, D), jnp.bfloat16)])

    def expert_step(carry, inputs):
        accum, products = carry
        slots, gate_up_weight, down_weight = inputs
        token = slots // TOP
        rows = pad_rows[token]
        grad_rows = pad_grads[token]
        output, d_rows = expert_pass(rows, grad_rows, gate_up_weight, down_weight)
        dots = lax.optimization_barrier(jnp.sum(grad_rows.astype(jnp.float32) * output.astype(jnp.float32), axis=-1))
        accum = accum.at[token].add(weights[slots][:, None] * d_rows.astype(jnp.float32))
        products = products.at[slots].set(dots)
        return ((accum, products), None)
    start = (jnp.zeros((total_rows + 1, D), jnp.float32), jnp.zeros((total_rows * TOP + 1,), jnp.float32))
    (accum, products), _ = lax.scan(expert_step, start, (table, w_gate_up, w_down))
    d_normed = accum[:total_rows]
    d_values = jax.vjp(lambda inner: normalize(inner, norm_gain), values)[1](d_normed)[0]
    grad_x = (grads.astype(jnp.float32) + d_values).astype(jnp.bfloat16).reshape(GROUPS, TOKENS, D)
    grad_w = products[:total_rows * TOP].reshape(GROUPS, TOKENS, TOP).astype(jnp.bfloat16)
    return (grad_x, grad_w)
```

```python
import math

import jax
import jax.numpy as jnp
import numpy as np
from jax import lax
from jax.sharding import PartitionSpec as P

NFFT = 400
HOP = 160
TIME = 64
MEL_FLOOR = 0.1
EPS_LAYER = 1e-05
EPS_ROOT = 1e-06
SAMPLE_RATE = 16000.0
CAP = 20
HEAD = 16
TAIL = CAP - HEAD
HIGHEST = lax.Precision.HIGHEST


def mel_scale(frequency):
    frequency = np.asarray(frequency) * 1.0
    log_part = 15.0 + np.log(np.maximum(frequency, 1000.0) / 1000.0) * 27.0 / math.log(6.4)
    return np.where(frequency < 1000.0, frequency * 3.0 / 200.0, log_part)


def mel_inverse(levels):
    levels = np.asarray(levels) * 1.0
    log_part = 1000.0 * np.exp((np.maximum(levels, 15.0) - 15.0) * math.log(6.4) / 27.0)
    return np.where(levels < 15.0, levels * 200.0 / 3.0, log_part)


def mel_table(bins_count, mel_count, frame_size):
    edges = mel_inverse(np.linspace(0.0, float(mel_scale(SAMPLE_RATE / 2.0)), mel_count + 2))
    centers = (np.arange(bins_count) * 1.0)[:, None] * SAMPLE_RATE / frame_size
    lower = edges[:-2][None, :]
    middle = edges[1:-1][None, :]
    upper = edges[2:][None, :]
    rising = (centers - lower) / (middle - lower)
    falling = (upper - centers) / (upper - middle)
    return np.maximum(0.0, np.minimum(rising, falling))


def dft_windowed(count, bins_count):
    sample = np.arange(count)[:, None]
    frequency = np.arange(bins_count)[None, :]
    angle = 2.0 * np.pi * ((sample * frequency) % count) / count
    window = (0.5 - 0.5 * np.cos(2.0 * np.pi * np.arange(count) / count))[:, None]
    table = np.zeros((count, 512))
    table[:, :bins_count] = window * np.cos(angle)
    table[:, 256 : 256 + bins_count] = -window * np.sin(angle)
    return table.astype(np.float32)


def sinusoid_table(count, width):
    half = width // 2
    rates = np.exp(-math.log(10000.0) * np.arange(half) / (half - 1))
    angles = np.arange(count)[:, None] * rates[None, :]
    return np.concatenate([np.sin(angles), np.cos(angles)], axis=1).astype(np.float32)


def layer_norm(values):
    centered = values - jnp.mean(values, axis=-1, keepdims=True)
    return centered * lax.rsqrt(jnp.mean(centered * centered, axis=-1, keepdims=True) + EPS_LAYER)


def normalize(values, gain):
    return values * lax.rsqrt(jnp.mean(values * values, axis=-1, keepdims=True) + EPS_ROOT) * gain


def dot(left, right):
    return jnp.dot(left, right, preferred_element_type=jnp.float32)


def swap(value):
    return lax.ppermute(value, "dp", [(0, 1), (1, 0)])


def send_head(rows):
    width = rows.shape[-1]
    out = lax.all_to_all(
        rows.reshape(-1, HEAD, width), ("section", "ep"), split_axis=0, concat_axis=0, tiled=True
    )
    return out.reshape(-1, width)


def send_tail(rows):
    width = rows.shape[-1]
    part = width // 4
    packed = rows.reshape(-1, TAIL, 4, part).transpose(0, 2, 1, 3).reshape(-1, 4 * TAIL, part)
    out = lax.all_to_all(packed, ("section", "ep"), split_axis=0, concat_axis=0, tiled=True)
    return out.reshape(-1, 4, TAIL, part).transpose(0, 2, 1, 3).reshape(-1, width)


def exchange(rows, experts):
    head = experts * HEAD
    return jnp.concatenate([send_head(rows[:head]), send_tail(rows[head:])], axis=0)


def shards(
    samples,
    req_frames,
    w_in,
    w_up_aud,
    w_down_aud,
    w_out,
    norm_gain,
    expert_ids,
    gate_weights,
    cotangent,
    w_gate_up,
    w_down,
):
    local_rows = samples[0]
    request_total, slab, hop = local_rows.shape
    grads = cotangent[0]
    tokens, width = grads.shape
    experts = lax.axis_size("section") * lax.axis_size("ep")
    senders = lax.axis_size("ep")
    requests = request_total // senders

    arrived = lax.all_to_all(
        local_rows.reshape(senders, requests * slab, hop),
        "ep",
        split_axis=0,
        concat_axis=0,
        tiled=True,
    ).reshape(-1, hop)

    ids = expert_ids[0].T
    names = ids[:, None, :] == jnp.arange(experts, dtype=jnp.int32)[None, :, None]
    member = jnp.any(names, axis=0)
    before = jnp.asarray(np.triu(np.ones((tokens, tokens)), 1), jnp.bfloat16)
    rank = dot(member.astype(jnp.bfloat16), before).astype(jnp.int32)
    rank = jnp.where(member, rank, -1)
    head_slots = rank[:, None, :] == jnp.arange(HEAD, dtype=jnp.int32)[None, :, None]
    tail_slots = rank[:, None, :] == jnp.arange(HEAD, CAP, dtype=jnp.int32)[None, :, None]
    slots = jnp.concatenate(
        [head_slots.reshape(-1, tokens), tail_slots.reshape(-1, tokens)], axis=0
    )
    picks = slots.astype(jnp.bfloat16)
    send_grads = dot(picks, grads).astype(jnp.bfloat16)
    arrived_grads = exchange(send_grads, experts)

    lengths = req_frames[0, 0]
    ends = jnp.cumsum(lengths)
    places = jnp.arange(tokens, dtype=jnp.int32)
    later = places[:, None] >= ends[None, :-1]
    request = jnp.sum(later.astype(jnp.int32), axis=-1)
    times = places - jnp.sum(jnp.where(later, lengths[None, :-1], 0), axis=-1)
    parts = []
    for offset in range(3):
        at = times + offset
        row = jnp.where(at < TIME, (at // slab) * (requests * slab) + request * slab + at % slab, -1)
        pick = (row[:, None] == jnp.arange(arrived.shape[0], dtype=jnp.int32)).astype(jnp.float32)
        parts.append(jnp.dot(pick, arrived, precision=HIGHEST, preferred_element_type=jnp.float32))
    frames = jnp.concatenate(parts, axis=-1)[:, :NFFT]

    bins_count = NFFT // 2 + 1
    spectrum = jnp.dot(
        frames,
        jnp.asarray(dft_windowed(NFFT, bins_count)),
        precision=HIGHEST,
        preferred_element_type=jnp.float32,
    )
    power = spectrum[:, :256] ** 2 + spectrum[:, 256:] ** 2
    table = np.zeros((256, w_in.shape[0]), np.float32)
    table[:bins_count] = mel_table(bins_count, w_in.shape[0], NFFT)
    energy = jnp.dot(
        power, jnp.asarray(table), precision=HIGHEST, preferred_element_type=jnp.float32
    )
    log_mel = jnp.log(jnp.maximum(energy, MEL_FLOOR)).astype(jnp.bfloat16)
    time_pick = (times[:, None] == jnp.arange(TIME, dtype=jnp.int32)).astype(jnp.float32)
    position = jnp.dot(
        time_pick,
        jnp.asarray(sinusoid_table(TIME, w_in.shape[1])),
        precision=HIGHEST,
        preferred_element_type=jnp.float32,
    )
    state = dot(log_mel, w_in) + position
    normed_audio = layer_norm(state).astype(jnp.bfloat16)

    def half_product(values):
        hidden = jax.nn.gelu(dot(values, w_up_aud), approximate=False).astype(jnp.bfloat16)
        return dot(hidden, w_down_aud)

    other = swap(normed_audio)
    theirs = half_product(other).astype(jnp.bfloat16)
    ours = half_product(normed_audio)
    encoded = state + (ours + swap(theirs).astype(jnp.float32))
    final_audio = layer_norm(encoded).astype(jnp.bfloat16)
    values = dot(final_audio, w_out).astype(jnp.bfloat16).astype(jnp.float32)
    normed = normalize(values, norm_gain).astype(jnp.bfloat16)

    normed, arrived_grads = lax.optimization_barrier((normed, arrived_grads))
    arrived_rows = exchange(dot(picks, normed).astype(jnp.bfloat16), experts)

    gate_up = w_gate_up[0]
    down = w_down[0]
    hidden_count = down.shape[0]
    back = dot(arrived_grads, down.T)
    both = dot(arrived_rows, gate_up)
    gate = both[:, :hidden_count]
    upper = both[:, hidden_count:]
    sigma = jax.nn.sigmoid(gate)
    active = (gate * sigma * upper).astype(jnp.bfloat16).astype(jnp.float32)
    products = jnp.sum(active * back, axis=-1)
    d_gate = back * upper * sigma * (1.0 + gate * (1.0 - sigma))
    d_upper = back * gate * sigma
    d_both = jnp.concatenate([d_gate, d_upper], axis=1).astype(jnp.bfloat16)
    d_rows = dot(d_both, gate_up.T).astype(jnp.bfloat16)

    head = experts * HEAD
    scalars = jnp.concatenate(
        [products[:head].reshape(experts, HEAD), products[head:].reshape(experts, TAIL)], axis=1
    )
    scalars = jnp.pad(scalars, ((0, 0), (0, 128 - CAP)))
    scalars = lax.all_to_all(
        scalars, ("section", "ep"), split_axis=0, concat_axis=0, tiled=True
    )[:, :CAP]
    returned = exchange(d_rows, experts)

    weight = jnp.sum(jnp.where(names, gate_weights[0].T[:, None, :], 0.0), axis=0)
    spread = jnp.where(
        slots,
        jnp.concatenate(
            [
                jnp.broadcast_to(weight[:, None, :], (experts, HEAD, tokens)).reshape(-1, tokens),
                jnp.broadcast_to(weight[:, None, :], (experts, TAIL, tokens)).reshape(-1, tokens),
            ],
            axis=0,
        ),
        0.0,
    )
    coarse = spread.astype(jnp.bfloat16)
    fine = (spread - coarse.astype(jnp.float32)).astype(jnp.bfloat16)
    both_weights = jnp.concatenate([coarse, fine], axis=1)
    sums = lax.dot_general(
        both_weights, returned, (((0,), (0,)), ((), ())), preferred_element_type=jnp.float32
    )
    d_normed = sums[:tokens] + sums[tokens:]
    d_values = jax.vjp(lambda inner: normalize(inner, norm_gain), values)[1](d_normed)[0]
    grad_x = (grads.astype(jnp.float32) + d_values).astype(jnp.bfloat16)

    seat = rank[:, None, :] == jnp.arange(CAP, dtype=jnp.int32)[None, :, None]
    by_token = jnp.sum(jnp.where(seat, scalars[:, :, None], 0.0), axis=1)
    grad_w = jnp.sum(jnp.where(names, by_token[None], 0.0), axis=1).T.astype(jnp.bfloat16)
    return (grad_x[None], grad_w[None])


def solution(mesh):
    in_specs = (
        P(("section", "dp"), None, "ep", None),
        P(("section", "dp"), "ep", None),
        P(),
        P(None, "dp"),
        P("dp", None),
        P(),
        P(),
        P(("section", "dp"), "ep", None),
        P(("section", "dp"), "ep", None),
        P(("section", "dp"), "ep", None),
        P(("section", "ep"), None, None),
        P(("section", "ep"), None, None),
    )
    out_specs = (P(("section", "dp"), "ep", None), P(("section", "dp"), "ep", None))
    return jax.shard_map(shards, mesh=mesh, in_specs=in_specs, out_specs=out_specs, check_vma=False)
```

```python
import math

import jax
import jax.numpy as jnp
import numpy as np
from jax import lax
from jax.experimental import pallas as pl
from jax.experimental.pallas import tpu as pltpu
from jax.sharding import PartitionSpec as P

NFFT = 400
HOP = 160
TIME = 64
MEL_FLOOR = 0.1
EPS_LAYER = 1e-05
EPS_ROOT = 1e-06
SAMPLE_RATE = 16000.0
CAP = 20
HEAD = 16
TAIL = CAP - HEAD
WIDTH = 2048
PART = WIDTH // 4
HIGHEST = lax.Precision.HIGHEST


def mel_scale(frequency):
    frequency = np.asarray(frequency) * 1.0
    log_part = 15.0 + np.log(np.maximum(frequency, 1000.0) / 1000.0) * 27.0 / math.log(6.4)
    return np.where(frequency < 1000.0, frequency * 3.0 / 200.0, log_part)


def mel_inverse(levels):
    levels = np.asarray(levels) * 1.0
    log_part = 1000.0 * np.exp((np.maximum(levels, 15.0) - 15.0) * math.log(6.4) / 27.0)
    return np.where(levels < 15.0, levels * 200.0 / 3.0, log_part)


def mel_table(bins_count, mel_count, frame_size):
    edges = mel_inverse(np.linspace(0.0, float(mel_scale(SAMPLE_RATE / 2.0)), mel_count + 2))
    centers = (np.arange(bins_count) * 1.0)[:, None] * SAMPLE_RATE / frame_size
    lower = edges[:-2][None, :]
    middle = edges[1:-1][None, :]
    upper = edges[2:][None, :]
    rising = (centers - lower) / (middle - lower)
    falling = (upper - centers) / (upper - middle)
    return np.maximum(0.0, np.minimum(rising, falling))


def dft_windowed(count, bins_count):
    sample = np.arange(count)[:, None]
    frequency = np.arange(bins_count)[None, :]
    angle = 2.0 * np.pi * ((sample * frequency) % count) / count
    window = (0.5 - 0.5 * np.cos(2.0 * np.pi * np.arange(count) / count))[:, None]
    table = np.zeros((count, 512))
    table[:, :bins_count] = window * np.cos(angle)
    table[:, 256 : 256 + bins_count] = -window * np.sin(angle)
    return table.astype(np.float32)


def sinusoid_table(count, width):
    half = width // 2
    rates = np.exp(-math.log(10000.0) * np.arange(half) / (half - 1))
    angles = np.arange(count)[:, None] * rates[None, :]
    return np.concatenate([np.sin(angles), np.cos(angles)], axis=1).astype(np.float32)


def layer_norm(values):
    centered = values - jnp.mean(values, axis=-1, keepdims=True)
    return centered * lax.rsqrt(jnp.mean(centered * centered, axis=-1, keepdims=True) + EPS_LAYER)


def normalize(values, gain):
    return values * lax.rsqrt(jnp.mean(values * values, axis=-1, keepdims=True) + EPS_ROOT) * gain


def dot(left, right):
    return jnp.dot(left, right, preferred_element_type=jnp.float32)


def swap(value):
    return lax.ppermute(value, "dp", [(0, 1), (1, 0)])


def exchange(rows):
    width = rows.shape[-1]
    out = lax.all_to_all(
        rows.reshape(-1, HEAD, width), ("section", "ep"), split_axis=0, concat_axis=0, tiled=True
    )
    return out.reshape(-1, width)


def quarter_of(shape, axis=0):
    return lax.rem(lax.broadcasted_iota(jnp.int32, shape, axis), HEAD) // TAIL


def pack_body(head_ref, tail_ref, values_ref, out_ref):
    out_ref[:, :WIDTH] = dot(head_ref[...], values_ref[...]).astype(jnp.bfloat16)
    quarter = quarter_of((head_ref.shape[0], PART))
    packed = jnp.zeros(quarter.shape, jnp.float32)
    for q in range(4):
        piece = dot(tail_ref[...], values_ref[:, q * PART : (q + 1) * PART])
        packed = jnp.where(quarter == q, piece, packed)
    out_ref[:, WIDTH:] = packed.astype(jnp.bfloat16)


def pack(head_picks, tail_picks, values):
    rows, tokens = head_picks.shape
    block = rows // 4
    return pl.pallas_call(
        pack_body,
        grid=(4,),
        in_specs=[
            pl.BlockSpec((block, tokens), lambda i: (i, 0)),
            pl.BlockSpec((block, tokens), lambda i: (i, 0)),
            pl.BlockSpec((tokens, WIDTH), lambda i: (0, 0)),
        ],
        out_specs=pl.BlockSpec((block, WIDTH + PART), lambda i: (i, 0)),
        out_shape=jax.ShapeDtypeStruct((rows, WIDTH + PART), jnp.bfloat16),
        cost_estimate=pl.CostEstimate(
            flops=4 * rows * tokens * WIDTH, bytes_accessed=6_500_000, transcendentals=0
        ),
        name="pack_slots",
    )(head_picks, tail_picks, values)


def contract_last(left, right):
    return lax.dot_general(
        left, right, (((1,), (1,)), ((), ())), preferred_element_type=jnp.float32
    )


def expert_body(rows_ref, grads_ref, gate_up_ref, down_ref, out_ref, full_ref):
    head = rows_ref.shape[0]
    tail = head // 4
    hidden_count = down_ref.shape[0]
    to = lax.broadcasted_iota(jnp.int32, (tail, head), 0)
    at = lax.broadcasted_iota(jnp.int32, (tail, head), 1)
    base = (to // TAIL) * HEAD + lax.rem(to, TAIL)

    def unpack(ref):
        full_ref[:head, :] = ref[:, :WIDTH]
        for q in range(4):
            gather = jnp.where(at == base + q * TAIL, 1.0, 0.0).astype(jnp.bfloat16)
            full_ref[head:, q * PART : (q + 1) * PART] = dot(gather, ref[:, WIDTH:]).astype(
                jnp.bfloat16
            )

    unpack(grads_ref)
    back = contract_last(full_ref[...], down_ref[...])
    unpack(rows_ref)
    both = dot(full_ref[...], gate_up_ref[...])
    gate = both[:, :hidden_count]
    upper = both[:, hidden_count:]
    sigma = jax.nn.sigmoid(gate)
    active = (gate * sigma * upper).astype(jnp.bfloat16).astype(jnp.float32)
    products = jnp.sum(active * back, axis=1, keepdims=True)
    d_gate = back * upper * sigma * (1.0 + gate * (1.0 - sigma))
    d_upper = back * gate * sigma
    d_both = jnp.concatenate([d_gate.astype(jnp.bfloat16), d_upper.astype(jnp.bfloat16)], axis=1)
    d_rows = contract_last(d_both, gate_up_ref[...]).astype(jnp.bfloat16)
    out_ref[:, :WIDTH] = d_rows[:head]
    row = lax.broadcasted_iota(jnp.int32, (head, tail), 0)
    column = lax.broadcasted_iota(jnp.int32, (head, tail), 1)
    source = (row // HEAD) * TAIL + lax.rem(row, TAIL)
    scatter = jnp.where(column == source, 1.0, 0.0).astype(jnp.bfloat16)
    quarter = quarter_of((head, PART))
    packed = jnp.zeros((head, PART), jnp.float32)
    for q in range(4):
        piece = dot(scatter, d_rows[head:, q * PART : (q + 1) * PART])
        packed = jnp.where(quarter == q, piece, packed)
    out_ref[:, WIDTH : WIDTH + PART] = packed.astype(jnp.bfloat16)
    wide = jnp.broadcast_to(products, (head + tail, 128))
    tail_wide = dot(scatter, wide[head:].astype(jnp.bfloat16))
    lane = lax.broadcasted_iota(jnp.int32, (head, 128), 1)
    out_ref[:, WIDTH + PART :] = jnp.where(lane < 64, wide[:head], tail_wide).astype(jnp.bfloat16)


def experts_run(rows, grads, gate_up, down):
    total = rows.shape[0]
    block = total // 4
    full = lambda i: (0, 0)
    return pl.pallas_call(
        expert_body,
        grid=(4,),
        in_specs=[
            pl.BlockSpec((block, WIDTH + PART), lambda i: (i, 0)),
            pl.BlockSpec((block, WIDTH + PART), lambda i: (i, 0)),
            pl.BlockSpec(gate_up.shape, full),
            pl.BlockSpec(down.shape, full),
        ],
        out_specs=pl.BlockSpec((block, WIDTH + PART + 128), lambda i: (i, 0)),
        out_shape=jax.ShapeDtypeStruct((total, WIDTH + PART + 128), jnp.bfloat16),
        scratch_shapes=[pltpu.VMEM((block + block // 4, WIDTH), jnp.bfloat16)],
        compiler_params=pltpu.CompilerParams(vmem_limit_bytes=62_000_000),
        cost_estimate=pl.CostEstimate(
            flops=20_000_000_000, bytes_accessed=25_000_000, transcendentals=1_000_000
        ),
        name="experts",
    )(rows, grads, gate_up, down)


def combine_body(head_ref, tail_ref, rows_ref, out_ref):
    tokens = out_ref.shape[0]

    def split(value):
        coarse = value.astype(jnp.bfloat16)
        fine = (value - coarse.astype(jnp.float32)).astype(jnp.bfloat16)
        return jnp.concatenate([coarse, fine], axis=0)

    head = split(head_ref[...])
    quarter = quarter_of(tail_ref.shape, 1)
    for q in range(4):
        columns = pl.ds(q * PART, PART)
        weights = split(jnp.where(quarter == q, tail_ref[...], 0.0))
        total = dot(head, rows_ref[:, columns]) + dot(weights, rows_ref[:, WIDTH : WIDTH + PART])
        out_ref[:, columns] = total[:tokens] + total[tokens:]


def combine(head_weights, tail_weights, rows):
    return pl.pallas_call(
        combine_body,
        out_shape=jax.ShapeDtypeStruct((head_weights.shape[0], WIDTH), jnp.float32),
        name="combine",
    )(head_weights, tail_weights, rows)


def shards(
    samples,
    req_frames,
    w_in,
    w_up_aud,
    w_down_aud,
    w_out,
    norm_gain,
    expert_ids,
    gate_weights,
    cotangent,
    w_gate_up,
    w_down,
):
    local_rows = samples[0]
    request_total, slab, hop = local_rows.shape
    grads = cotangent[0]
    tokens, width = grads.shape
    experts = lax.axis_size("section") * lax.axis_size("ep")
    senders = lax.axis_size("ep")
    requests = request_total // senders

    arrived = lax.all_to_all(
        local_rows.reshape(senders, requests * slab, hop),
        "ep",
        split_axis=0,
        concat_axis=0,
        tiled=True,
    ).reshape(-1, hop)

    ids = expert_ids[0].T
    names = ids[:, None, :] == jnp.arange(experts, dtype=jnp.int32)[None, :, None]
    member = jnp.any(names, axis=0)
    before = jnp.asarray(np.triu(np.ones((tokens, tokens)), 1), jnp.bfloat16)
    rank = dot(member.astype(jnp.bfloat16), before).astype(jnp.int32)
    rank = jnp.where(member, rank, -1)
    place = jnp.arange(HEAD, dtype=jnp.int32)[None, :, None]
    head_slots = (rank[:, None, :] == place).reshape(-1, tokens)
    tail_slots = (rank[:, None, :] == HEAD + place % TAIL).reshape(-1, tokens)
    head_picks = head_slots.astype(jnp.bfloat16)
    tail_picks = tail_slots.astype(jnp.bfloat16)
    arrived_grads = exchange(pack(head_picks, tail_picks, grads))

    lengths = req_frames[0, 0]
    ends = jnp.cumsum(lengths)
    places = jnp.arange(tokens, dtype=jnp.int32)
    later = places[:, None] >= ends[None, :-1]
    request = jnp.sum(later.astype(jnp.int32), axis=-1)
    times = places - jnp.sum(jnp.where(later, lengths[None, :-1], 0), axis=-1)
    parts = []
    for offset in range(3):
        at = times + offset
        row = jnp.where(at < TIME, (at // slab) * (requests * slab) + request * slab + at % slab, -1)
        pick = (row[:, None] == jnp.arange(arrived.shape[0], dtype=jnp.int32)).astype(jnp.float32)
        parts.append(jnp.dot(pick, arrived, precision=HIGHEST, preferred_element_type=jnp.float32))
    frames = jnp.concatenate(parts, axis=-1)[:, :NFFT]

    bins_count = NFFT // 2 + 1
    spectrum = jnp.dot(
        frames,
        jnp.asarray(dft_windowed(NFFT, bins_count)),
        precision=HIGHEST,
        preferred_element_type=jnp.float32,
    )
    power = spectrum[:, :256] ** 2 + spectrum[:, 256:] ** 2
    table = np.zeros((256, w_in.shape[0]), np.float32)
    table[:bins_count] = mel_table(bins_count, w_in.shape[0], NFFT)
    energy = jnp.dot(
        power, jnp.asarray(table), precision=HIGHEST, preferred_element_type=jnp.float32
    )
    log_mel = jnp.log(jnp.maximum(energy, MEL_FLOOR)).astype(jnp.bfloat16)
    time_pick = (times[:, None] == jnp.arange(TIME, dtype=jnp.int32)).astype(jnp.float32)
    position = jnp.dot(
        time_pick,
        jnp.asarray(sinusoid_table(TIME, w_in.shape[1])),
        precision=HIGHEST,
        preferred_element_type=jnp.float32,
    )
    state = dot(log_mel, w_in) + position
    normed_audio = layer_norm(state).astype(jnp.bfloat16)

    def half_product(values):
        hidden = jax.nn.gelu(dot(values, w_up_aud), approximate=False).astype(jnp.bfloat16)
        return dot(hidden, w_down_aud)

    other = swap(normed_audio)
    theirs = half_product(other).astype(jnp.bfloat16)
    ours = half_product(normed_audio)
    encoded = state + (ours + swap(theirs).astype(jnp.float32))
    final_audio = layer_norm(encoded).astype(jnp.bfloat16)
    values = dot(final_audio, w_out).astype(jnp.bfloat16).astype(jnp.float32)
    normed = normalize(values, norm_gain).astype(jnp.bfloat16)

    normed, arrived_grads = lax.optimization_barrier((normed, arrived_grads))
    arrived_rows = exchange(pack(head_picks, tail_picks, normed))
    returned = exchange(experts_run(arrived_rows, arrived_grads, w_gate_up[0], w_down[0]))

    weight = jnp.sum(jnp.where(names, gate_weights[0].T[:, None, :], 0.0), axis=0)
    weight = jnp.broadcast_to(weight[:, None, :], (experts, HEAD, tokens)).reshape(-1, tokens)
    d_normed = combine(
        jnp.where(head_slots, weight, 0.0).T, jnp.where(tail_slots, weight, 0.0).T, returned
    )
    d_values = jax.vjp(lambda inner: normalize(inner, norm_gain), values)[1](d_normed)[0]
    grad_x = (grads.astype(jnp.float32) + d_values).astype(jnp.bfloat16)

    scalars = returned[:, WIDTH + PART :].astype(jnp.float32)
    first = (jnp.arange(experts * HEAD) % HEAD < TAIL)[:, None]
    picked = jnp.where(head_slots, scalars[:, :1], 0.0)
    picked = picked + jnp.where(tail_slots & first, scalars[:, 64:65], 0.0)
    by_token = jnp.sum(picked.reshape(experts, HEAD, tokens), axis=1)
    grad_w = jnp.sum(jnp.where(names, by_token[None], 0.0), axis=1).T.astype(jnp.bfloat16)
    return (grad_x[None], grad_w[None])


def solution(mesh):
    in_specs = (
        P(("section", "dp"), None, "ep", None),
        P(("section", "dp"), "ep", None),
        P(),
        P(None, "dp"),
        P("dp", None),
        P(),
        P(),
        P(("section", "dp"), "ep", None),
        P(("section", "dp"), "ep", None),
        P(("section", "dp"), "ep", None),
        P(("section", "ep"), None, None),
        P(("section", "ep"), None, None),
    )
    out_specs = (P(("section", "dp"), "ep", None), P(("section", "dp"), "ep", None))
    return jax.shard_map(shards, mesh=mesh, in_specs=in_specs, out_specs=out_specs, check_vma=False)
```

```python
import functools
import math

import jax
import jax.numpy as jnp
import numpy as np
from jax import lax
from jax.experimental import pallas as pl
from jax.experimental.pallas import tpu as pltpu
from jax.sharding import PartitionSpec as P

NFFT = 400
HOP = 160
TIME = 64
MEL_FLOOR = 0.1
EPS_LAYER = 1e-05
EPS_ROOT = 1e-06
SAMPLE_RATE = 16000.0
CAP = 20
HEAD = 16
TAIL = CAP - HEAD
WIDTH = 2048
PART = WIDTH // 4
SPLIT = 1024
HIGHEST = lax.Precision.HIGHEST


def mel_scale(frequency):
    frequency = np.asarray(frequency) * 1.0
    log_part = 15.0 + np.log(np.maximum(frequency, 1000.0) / 1000.0) * 27.0 / math.log(6.4)
    return np.where(frequency < 1000.0, frequency * 3.0 / 200.0, log_part)


def mel_inverse(levels):
    levels = np.asarray(levels) * 1.0
    log_part = 1000.0 * np.exp((np.maximum(levels, 15.0) - 15.0) * math.log(6.4) / 27.0)
    return np.where(levels < 15.0, levels * 200.0 / 3.0, log_part)


def mel_table(bins_count, mel_count, frame_size):
    edges = mel_inverse(np.linspace(0.0, float(mel_scale(SAMPLE_RATE / 2.0)), mel_count + 2))
    centers = (np.arange(bins_count) * 1.0)[:, None] * SAMPLE_RATE / frame_size
    lower = edges[:-2][None, :]
    middle = edges[1:-1][None, :]
    upper = edges[2:][None, :]
    rising = (centers - lower) / (middle - lower)
    falling = (upper - centers) / (upper - middle)
    return np.maximum(0.0, np.minimum(rising, falling))


def dft_windowed(count, bins_count):
    sample = np.arange(count)[:, None]
    frequency = np.arange(bins_count)[None, :]
    angle = 2.0 * np.pi * ((sample * frequency) % count) / count
    window = (0.5 - 0.5 * np.cos(2.0 * np.pi * np.arange(count) / count))[:, None]
    table = np.zeros((count, 512))
    table[:, :bins_count] = window * np.cos(angle)
    table[:, 256 : 256 + bins_count] = -window * np.sin(angle)
    return table.astype(np.float32)


def sinusoid_table(count, width):
    half = width // 2
    rates = np.exp(-math.log(10000.0) * np.arange(half) / (half - 1))
    angles = np.arange(count)[:, None] * rates[None, :]
    return np.concatenate([np.sin(angles), np.cos(angles)], axis=1).astype(np.float32)


def layer_norm(values):
    centered = values - jnp.mean(values, axis=-1, keepdims=True)
    return centered * lax.rsqrt(jnp.mean(centered * centered, axis=-1, keepdims=True) + EPS_LAYER)


def normalize(values, gain):
    return values * lax.rsqrt(jnp.mean(values * values, axis=-1, keepdims=True) + EPS_ROOT) * gain


def dot(left, right):
    return jnp.dot(left, right, preferred_element_type=jnp.float32)


def swap(value):
    return lax.ppermute(value, "dp", [(0, 1), (1, 0)])


def exchange(rows):
    width = rows.shape[-1]
    out = lax.all_to_all(
        rows.reshape(-1, HEAD, width), ("section", "ep"), split_axis=0, concat_axis=0, tiled=True
    )
    return out.reshape(-1, width)


def quarter_of(shape, axis=0):
    return lax.rem(lax.broadcasted_iota(jnp.int32, shape, axis), HEAD) // TAIL


def pack_body(split, head_ref, tail_ref, values_ref, *out_refs):
    head = dot(head_ref[...], values_ref[...]).astype(jnp.bfloat16)
    quarter = quarter_of((head_ref.shape[0], PART))
    packed = jnp.zeros(quarter.shape, jnp.float32)
    for q in range(4):
        piece = dot(tail_ref[...], values_ref[:, q * PART : (q + 1) * PART])
        packed = jnp.where(quarter == q, piece, packed)
    if split:
        out_refs[0][...] = head[:, :split]
    out_refs[-1][:, : WIDTH - split] = head[:, split:]
    out_refs[-1][:, WIDTH - split :] = packed.astype(jnp.bfloat16)


def pack(head_picks, tail_picks, values, split=0):
    rows, tokens = head_picks.shape
    block = rows // 4
    widths = ([split] if split else []) + [WIDTH + PART - split]
    return pl.pallas_call(
        functools.partial(pack_body, split),
        grid=(4,),
        in_specs=[
            pl.BlockSpec((block, tokens), lambda i: (i, 0)),
            pl.BlockSpec((block, tokens), lambda i: (i, 0)),
            pl.BlockSpec((tokens, WIDTH), lambda i: (0, 0)),
        ],
        out_specs=[pl.BlockSpec((block, width), lambda i: (i, 0)) for width in widths],
        out_shape=[jax.ShapeDtypeStruct((rows, width), jnp.bfloat16) for width in widths],
        cost_estimate=pl.CostEstimate(
            flops=4 * rows * tokens * WIDTH, bytes_accessed=6_500_000, transcendentals=0
        ),
        name="pack_slots",
    )(head_picks, tail_picks, values)


def contract_last(left, right):
    return lax.dot_general(
        left, right, (((1,), (1,)), ((), ())), preferred_element_type=jnp.float32
    )


def unpack_tail(packed, full_ref):
    head = packed.shape[0]
    tail = head // 4
    to = lax.broadcasted_iota(jnp.int32, (tail, head), 0)
    at = lax.broadcasted_iota(jnp.int32, (tail, head), 1)
    base = (to // TAIL) * HEAD + lax.rem(to, TAIL)
    for q in range(4):
        gather = jnp.where(at == base + q * TAIL, 1.0, 0.0).astype(jnp.bfloat16)
        full_ref[head:, q * PART : (q + 1) * PART] = dot(gather, packed).astype(jnp.bfloat16)


def back_body(first_ref, second_ref, down_ref, out_ref, full_ref):
    head = first_ref.shape[0]
    full_ref[:head, :SPLIT] = first_ref[...]
    full_ref[:head, SPLIT:] = second_ref[:, : WIDTH - SPLIT]
    unpack_tail(second_ref[:, WIDTH - SPLIT :], full_ref)
    out_ref[...] = contract_last(full_ref[...], down_ref[...])


def back_run(first, second, down):
    total = first.shape[0]
    block = total // 4
    rows = block + block // 4
    return pl.pallas_call(
        back_body,
        grid=(4,),
        in_specs=[
            pl.BlockSpec((block, first.shape[1]), lambda i: (i, 0)),
            pl.BlockSpec((block, second.shape[1]), lambda i: (i, 0)),
            pl.BlockSpec(down.shape, lambda i: (0, 0)),
        ],
        out_specs=pl.BlockSpec((rows, down.shape[0]), lambda i: (i, 0)),
        out_shape=jax.ShapeDtypeStruct((4 * rows, down.shape[0]), jnp.float32),
        scratch_shapes=[pltpu.VMEM((rows, WIDTH), jnp.bfloat16)],
        cost_estimate=pl.CostEstimate(
            flops=4_500_000_000, bytes_accessed=13_000_000, transcendentals=0
        ),
        name="back",
    )(first, second, down)


def expert_body(rows_ref, back_ref, gate_up_ref, out_ref, full_ref):
    head = rows_ref.shape[0]
    tail = head // 4
    hidden_count = back_ref.shape[1]
    back = back_ref[...]
    full_ref[:head, :] = rows_ref[:, :WIDTH]
    unpack_tail(rows_ref[:, WIDTH:], full_ref)
    both = dot(full_ref[...], gate_up_ref[...])
    gate = both[:, :hidden_count]
    upper = both[:, hidden_count:]
    sigma = jax.nn.sigmoid(gate)
    active = (gate * sigma * upper).astype(jnp.bfloat16).astype(jnp.float32)
    products = jnp.sum(active * back, axis=1, keepdims=True)
    d_gate = back * upper * sigma * (1.0 + gate * (1.0 - sigma))
    d_upper = back * gate * sigma
    d_both = jnp.concatenate([d_gate.astype(jnp.bfloat16), d_upper.astype(jnp.bfloat16)], axis=1)
    d_rows = contract_last(d_both, gate_up_ref[...]).astype(jnp.bfloat16)
    out_ref[:, :WIDTH] = d_rows[:head]
    row = lax.broadcasted_iota(jnp.int32, (head, tail), 0)
    column = lax.broadcasted_iota(jnp.int32, (head, tail), 1)
    source = (row // HEAD) * TAIL + lax.rem(row, TAIL)
    scatter = jnp.where(column == source, 1.0, 0.0).astype(jnp.bfloat16)
    quarter = quarter_of((head, PART))
    packed = jnp.zeros((head, PART), jnp.float32)
    for q in range(4):
        piece = dot(scatter, d_rows[head:, q * PART : (q + 1) * PART])
        packed = jnp.where(quarter == q, piece, packed)
    out_ref[:, WIDTH : WIDTH + PART] = packed.astype(jnp.bfloat16)
    wide = jnp.broadcast_to(products, (head + tail, 128))
    tail_wide = dot(scatter, wide[head:].astype(jnp.bfloat16))
    lane = lax.broadcasted_iota(jnp.int32, (head, 128), 1)
    out_ref[:, WIDTH + PART :] = jnp.where(lane < 64, wide[:head], tail_wide).astype(jnp.bfloat16)


def experts_run(rows, back, gate_up):
    total = rows.shape[0]
    block = total // 4
    full = lambda i: (0, 0)
    return pl.pallas_call(
        expert_body,
        grid=(4,),
        in_specs=[
            pl.BlockSpec((block, WIDTH + PART), lambda i: (i, 0)),
            pl.BlockSpec((block + block // 4, back.shape[1]), lambda i: (i, 0)),
            pl.BlockSpec(gate_up.shape, full),
        ],
        out_specs=pl.BlockSpec((block, WIDTH + PART + 128), lambda i: (i, 0)),
        out_shape=jax.ShapeDtypeStruct((total, WIDTH + PART + 128), jnp.bfloat16),
        scratch_shapes=[pltpu.VMEM((block + block // 4, WIDTH), jnp.bfloat16)],
        compiler_params=pltpu.CompilerParams(vmem_limit_bytes=62_000_000),
        cost_estimate=pl.CostEstimate(
            flops=16_000_000_000, bytes_accessed=25_000_000, transcendentals=1_000_000
        ),
        name="experts",
    )(rows, back, gate_up)


def combine_body(head_ref, tail_ref, rows_ref, out_ref):
    tokens = out_ref.shape[0]

    def split(value):
        coarse = value.astype(jnp.bfloat16)
        fine = (value - coarse.astype(jnp.float32)).astype(jnp.bfloat16)
        return jnp.concatenate([coarse, fine], axis=0)

    head = split(head_ref[...])
    quarter = quarter_of(tail_ref.shape, 1)

    @pl.loop(0, 4)
    def _(q):
        columns = pl.ds(pl.multiple_of(q * PART, PART), PART)
        weights = split(jnp.where(quarter == q, tail_ref[...], 0.0))
        total = dot(head, rows_ref[:, columns]) + dot(weights, rows_ref[:, WIDTH : WIDTH + PART])
        out_ref[:, columns] = total[:tokens] + total[tokens:]


def combine(head_weights, tail_weights, rows):
    return pl.pallas_call(
        combine_body,
        out_shape=jax.ShapeDtypeStruct((head_weights.shape[0], WIDTH), jnp.float32),
        name="combine",
    )(head_weights, tail_weights, rows)


def shards(
    samples,
    req_frames,
    w_in,
    w_up_aud,
    w_down_aud,
    w_out,
    norm_gain,
    expert_ids,
    gate_weights,
    cotangent,
    w_gate_up,
    w_down,
):
    local_rows = samples[0]
    request_total, slab, hop = local_rows.shape
    grads = cotangent[0]
    tokens, width = grads.shape
    experts = lax.axis_size("section") * lax.axis_size("ep")
    senders = lax.axis_size("ep")
    requests = request_total // senders

    arrived = lax.all_to_all(
        local_rows.reshape(senders, requests * slab, hop),
        "ep",
        split_axis=0,
        concat_axis=0,
        tiled=True,
    ).reshape(-1, hop)

    ids = expert_ids[0].T
    names = ids[:, None, :] == jnp.arange(experts, dtype=jnp.int32)[None, :, None]
    member = jnp.any(names, axis=0)
    before = jnp.asarray(np.triu(np.ones((tokens, tokens)), 1), jnp.bfloat16)
    rank = dot(member.astype(jnp.bfloat16), before).astype(jnp.int32)
    rank = jnp.where(member, rank, -1)
    place = jnp.arange(HEAD, dtype=jnp.int32)[None, :, None]
    head_slots = (rank[:, None, :] == place).reshape(-1, tokens)
    tail_slots = (rank[:, None, :] == HEAD + place % TAIL).reshape(-1, tokens)
    head_picks = head_slots.astype(jnp.bfloat16)
    tail_picks = tail_slots.astype(jnp.bfloat16)
    grads_first, grads_second = pack(head_picks, tail_picks, grads, SPLIT)
    arrived_first = exchange(grads_first)

    lengths = req_frames[0, 0]
    ends = jnp.cumsum(lengths)
    places = jnp.arange(tokens, dtype=jnp.int32)
    later = places[:, None] >= ends[None, :-1]
    request = jnp.sum(later.astype(jnp.int32), axis=-1)
    times = places - jnp.sum(jnp.where(later, lengths[None, :-1], 0), axis=-1)
    parts = []
    for offset in range(3):
        at = times + offset
        row = jnp.where(at < TIME, (at // slab) * (requests * slab) + request * slab + at % slab, -1)
        pick = (row[:, None] == jnp.arange(arrived.shape[0], dtype=jnp.int32)).astype(jnp.float32)
        parts.append(jnp.dot(pick, arrived, precision=HIGHEST, preferred_element_type=jnp.float32))
    frames = jnp.concatenate(parts, axis=-1)[:, :NFFT]

    bins_count = NFFT // 2 + 1
    spectrum = jnp.dot(
        frames,
        jnp.asarray(dft_windowed(NFFT, bins_count)),
        precision=HIGHEST,
        preferred_element_type=jnp.float32,
    )
    power = spectrum[:, :256] ** 2 + spectrum[:, 256:] ** 2
    table = np.zeros((256, w_in.shape[0]), np.float32)
    table[:bins_count] = mel_table(bins_count, w_in.shape[0], NFFT)
    energy = jnp.dot(
        power, jnp.asarray(table), precision=HIGHEST, preferred_element_type=jnp.float32
    )
    log_mel = jnp.log(jnp.maximum(energy, MEL_FLOOR)).astype(jnp.bfloat16)
    time_pick = (times[:, None] == jnp.arange(TIME, dtype=jnp.int32)).astype(jnp.float32)
    position = jnp.dot(
        time_pick,
        jnp.asarray(sinusoid_table(TIME, w_in.shape[1])),
        precision=HIGHEST,
        preferred_element_type=jnp.float32,
    )
    state = dot(log_mel, w_in) + position
    normed_audio = layer_norm(state).astype(jnp.bfloat16)

    def half_product(values):
        hidden = jax.nn.gelu(dot(values, w_up_aud), approximate=False).astype(jnp.bfloat16)
        return dot(hidden, w_down_aud)

    normed_audio, arrived_first = lax.optimization_barrier((normed_audio, arrived_first))
    other = swap(normed_audio)
    theirs = half_product(other).astype(jnp.bfloat16)
    ours = half_product(normed_audio)
    added = swap(theirs)
    grads_second, added = lax.optimization_barrier((grads_second, added))
    arrived_second = exchange(grads_second)
    encoded = state + (ours + added.astype(jnp.float32))
    final_audio = layer_norm(encoded).astype(jnp.bfloat16)
    values = dot(final_audio, w_out).astype(jnp.bfloat16).astype(jnp.float32)
    normed = normalize(values, norm_gain).astype(jnp.bfloat16)

    (packed,) = pack(head_picks, tail_picks, normed)
    packed, arrived_second = lax.optimization_barrier((packed, arrived_second))
    arrived_rows = exchange(packed)
    back = back_run(arrived_first, arrived_second, w_down[0])
    returned = exchange(experts_run(arrived_rows, back, w_gate_up[0]))

    weight = jnp.sum(jnp.where(names, gate_weights[0].T[:, None, :], 0.0), axis=0)
    weight = jnp.broadcast_to(weight[:, None, :], (experts, HEAD, tokens)).reshape(-1, tokens)
    d_normed = combine(
        jnp.where(head_slots, weight, 0.0).T, jnp.where(tail_slots, weight, 0.0).T, returned
    )
    d_values = jax.vjp(lambda inner: normalize(inner, norm_gain), values)[1](d_normed)[0]
    grad_x = (grads.astype(jnp.float32) + d_values).astype(jnp.bfloat16)

    scalars = returned[:, WIDTH + PART :].astype(jnp.float32)
    first = (jnp.arange(experts * HEAD) % HEAD < TAIL)[:, None]
    picked = jnp.where(head_slots, scalars[:, :1], 0.0)
    picked = picked + jnp.where(tail_slots & first, scalars[:, 64:65], 0.0)
    by_token = jnp.sum(picked.reshape(experts, HEAD, tokens), axis=1)
    grad_w = jnp.sum(jnp.where(names, by_token[None], 0.0), axis=1).T.astype(jnp.bfloat16)
    return (grad_x[None], grad_w[None])


def solution(mesh):
    in_specs = (
        P(("section", "dp"), None, "ep", None),
        P(("section", "dp"), "ep", None),
        P(),
        P(None, "dp"),
        P("dp", None),
        P(),
        P(),
        P(("section", "dp"), "ep", None),
        P(("section", "dp"), "ep", None),
        P(("section", "dp"), "ep", None),
        P(("section", "ep"), None, None),
        P(("section", "ep"), None, None),
    )
    out_specs = (P(("section", "dp"), "ep", None), P(("section", "dp"), "ep", None))
    return jax.shard_map(shards, mesh=mesh, in_specs=in_specs, out_specs=out_specs, check_vma=False)
```

```python
import functools
import math

import jax
import jax.numpy as jnp
import numpy as np
from jax import lax
from jax.experimental import pallas as pl
from jax.experimental.pallas import tpu as pltpu
from jax.sharding import PartitionSpec as P

NFFT = 400
HOP = 160
TIME = 64
MEL_FLOOR = 0.1
EPS_LAYER = 1e-05
EPS_ROOT = 1e-06
SAMPLE_RATE = 16000.0
CAP = 20
HEAD = 16
TAIL = CAP - HEAD
WIDTH = 2048
PART = WIDTH // 4
HIGHEST = lax.Precision.HIGHEST


def mel_scale(frequency):
    frequency = np.asarray(frequency) * 1.0
    log_part = 15.0 + np.log(np.maximum(frequency, 1000.0) / 1000.0) * 27.0 / math.log(6.4)
    return np.where(frequency < 1000.0, frequency * 3.0 / 200.0, log_part)


def mel_inverse(levels):
    levels = np.asarray(levels) * 1.0
    log_part = 1000.0 * np.exp((np.maximum(levels, 15.0) - 15.0) * math.log(6.4) / 27.0)
    return np.where(levels < 15.0, levels * 200.0 / 3.0, log_part)


def mel_table(bins_count, mel_count, frame_size):
    edges = mel_inverse(np.linspace(0.0, float(mel_scale(SAMPLE_RATE / 2.0)), mel_count + 2))
    centers = (np.arange(bins_count) * 1.0)[:, None] * SAMPLE_RATE / frame_size
    lower = edges[:-2][None, :]
    middle = edges[1:-1][None, :]
    upper = edges[2:][None, :]
    rising = (centers - lower) / (middle - lower)
    falling = (upper - centers) / (upper - middle)
    return np.maximum(0.0, np.minimum(rising, falling))


def dft_windowed(count, bins_count):
    sample = np.arange(count)[:, None]
    frequency = np.arange(bins_count)[None, :]
    angle = 2.0 * np.pi * ((sample * frequency) % count) / count
    window = (0.5 - 0.5 * np.cos(2.0 * np.pi * np.arange(count) / count))[:, None]
    table = np.zeros((count, 512))
    table[:, :bins_count] = window * np.cos(angle)
    table[:, 256 : 256 + bins_count] = -window * np.sin(angle)
    return table.astype(np.float32)


def sinusoid_table(count, width):
    half = width // 2
    rates = np.exp(-math.log(10000.0) * np.arange(half) / (half - 1))
    angles = np.arange(count)[:, None] * rates[None, :]
    return np.concatenate([np.sin(angles), np.cos(angles)], axis=1).astype(np.float32)


def layer_norm(values):
    centered = values - jnp.mean(values, axis=-1, keepdims=True)
    return centered * lax.rsqrt(jnp.mean(centered * centered, axis=-1, keepdims=True) + EPS_LAYER)


def normalize(values, gain):
    return values * lax.rsqrt(jnp.mean(values * values, axis=-1, keepdims=True) + EPS_ROOT) * gain


def dot(left, right):
    return jnp.dot(left, right, preferred_element_type=jnp.float32)


def swap(value):
    return lax.ppermute(value, "dp", [(0, 1), (1, 0)])


def exchange(rows):
    width = rows.shape[-1]
    out = lax.all_to_all(
        rows.reshape(-1, HEAD, width), ("section", "ep"), split_axis=0, concat_axis=0, tiled=True
    )
    return out.reshape(-1, width)


def quarter_of(shape, axis=0):
    return lax.rem(lax.broadcasted_iota(jnp.int32, shape, axis), HEAD) // TAIL


def pack_body(rank_ref, values_ref, out_ref):
    experts, tokens = rank_ref.shape
    rows = experts * HEAD
    rank = jnp.broadcast_to(rank_ref[...][:, None, :], (experts, HEAD, tokens))
    rank = rank.reshape(rows, tokens)
    place = lax.rem(lax.broadcasted_iota(jnp.int32, (rows, tokens), 0), HEAD)
    head = jnp.where(rank == place, 1.0, 0.0).astype(jnp.bfloat16)
    tail = jnp.where(rank == HEAD + lax.rem(place, TAIL), 1.0, 0.0).astype(jnp.bfloat16)
    out_ref[:, :WIDTH] = dot(head, values_ref[...]).astype(jnp.bfloat16)
    quarter = quarter_of((rows, PART))
    packed = jnp.zeros(quarter.shape, jnp.float32)
    for q in range(4):
        piece = dot(tail, values_ref[:, q * PART : (q + 1) * PART])
        packed = jnp.where(quarter == q, piece, packed)
    out_ref[:, WIDTH:] = packed.astype(jnp.bfloat16)


def pack(rank, values):
    experts, tokens = rank.shape
    block = experts // 4
    return pl.pallas_call(
        pack_body,
        grid=(4,),
        in_specs=[
            pl.BlockSpec((block, tokens), lambda i: (i, 0)),
            pl.BlockSpec((tokens, WIDTH), lambda i: (0, 0)),
        ],
        out_specs=pl.BlockSpec((block * HEAD, WIDTH + PART), lambda i: (i, 0)),
        out_shape=jax.ShapeDtypeStruct((experts * HEAD, WIDTH + PART), jnp.bfloat16),
        cost_estimate=pl.CostEstimate(
            flops=4 * experts * HEAD * tokens * WIDTH, bytes_accessed=6_500_000, transcendentals=0
        ),
        name="pack_slots",
    )(rank, values)


def contract_last(left, right):
    return lax.dot_general(
        left, right, (((1,), (1,)), ((), ())), preferred_element_type=jnp.float32
    )


def unpack_tail(packed, full_ref):
    head = packed.shape[0]
    tail = head // 4
    to = lax.broadcasted_iota(jnp.int32, (tail, head), 0)
    at = lax.broadcasted_iota(jnp.int32, (tail, head), 1)
    base = (to // TAIL) * HEAD + lax.rem(to, TAIL)
    for q in range(4):
        gather = jnp.where(at == base + q * TAIL, 1.0, 0.0).astype(jnp.bfloat16)
        full_ref[head:, q * PART : (q + 1) * PART] = dot(gather, packed).astype(jnp.bfloat16)


def back_body(grads_ref, down_ref, out_ref, full_ref):
    head = grads_ref.shape[0]
    full_ref[:head, :] = grads_ref[:, :WIDTH]
    unpack_tail(grads_ref[:, WIDTH:], full_ref)
    out_ref[...] = contract_last(full_ref[...], down_ref[...])


def back_run(grads, down):
    total = grads.shape[0]
    block = total // 4
    rows = block + block // 4
    return pl.pallas_call(
        back_body,
        grid=(4,),
        in_specs=[
            pl.BlockSpec((block, grads.shape[1]), lambda i: (i, 0)),
            pl.BlockSpec(down.shape, lambda i: (0, 0)),
        ],
        out_specs=pl.BlockSpec((rows, down.shape[0]), lambda i: (i, 0)),
        out_shape=jax.ShapeDtypeStruct((4 * rows, down.shape[0]), jnp.float32),
        scratch_shapes=[pltpu.VMEM((rows, WIDTH), jnp.bfloat16)],
        cost_estimate=pl.CostEstimate(
            flops=4_500_000_000, bytes_accessed=13_000_000, transcendentals=0
        ),
        name="back",
    )(grads, down)


def expert_body(rows_ref, back_ref, gate_up_ref, out_ref, full_ref):
    head = rows_ref.shape[0]
    tail = head // 4
    hidden_count = back_ref.shape[1]
    back = back_ref[...]
    full_ref[:head, :] = rows_ref[:, :WIDTH]
    unpack_tail(rows_ref[:, WIDTH:], full_ref)
    both = dot(full_ref[...], gate_up_ref[...])
    gate = both[:, :hidden_count]
    upper = both[:, hidden_count:]
    sigma = jax.nn.sigmoid(gate)
    active = (gate * sigma * upper).astype(jnp.bfloat16).astype(jnp.float32)
    products = jnp.sum(active * back, axis=1, keepdims=True)
    d_gate = back * upper * sigma * (1.0 + gate * (1.0 - sigma))
    d_upper = back * gate * sigma
    d_both = jnp.concatenate([d_gate.astype(jnp.bfloat16), d_upper.astype(jnp.bfloat16)], axis=1)
    d_rows = contract_last(d_both, gate_up_ref[...]).astype(jnp.bfloat16)
    out_ref[:, :WIDTH] = d_rows[:head]
    row = lax.broadcasted_iota(jnp.int32, (head, tail), 0)
    column = lax.broadcasted_iota(jnp.int32, (head, tail), 1)
    source = (row // HEAD) * TAIL + lax.rem(row, TAIL)
    scatter = jnp.where(column == source, 1.0, 0.0).astype(jnp.bfloat16)
    quarter = quarter_of((head, PART))
    packed = jnp.zeros((head, PART), jnp.float32)
    for q in range(4):
        piece = dot(scatter, d_rows[head:, q * PART : (q + 1) * PART])
        packed = jnp.where(quarter == q, piece, packed)
    out_ref[:, WIDTH : WIDTH + PART] = packed.astype(jnp.bfloat16)
    wide = jnp.broadcast_to(products, (head + tail, 128))
    tail_wide = dot(scatter, wide[head:].astype(jnp.bfloat16))
    lane = lax.broadcasted_iota(jnp.int32, (head, 128), 1)
    out_ref[:, WIDTH + PART :] = jnp.where(lane < 64, wide[:head], tail_wide).astype(jnp.bfloat16)


def experts_run(rows, back, gate_up):
    total = rows.shape[0]
    block = total // 4
    full = lambda i: (0, 0)
    return pl.pallas_call(
        expert_body,
        grid=(4,),
        in_specs=[
            pl.BlockSpec((block, WIDTH + PART), lambda i: (i, 0)),
            pl.BlockSpec((block + block // 4, back.shape[1]), lambda i: (i, 0)),
            pl.BlockSpec(gate_up.shape, full),
        ],
        out_specs=pl.BlockSpec((block, WIDTH + PART + 128), lambda i: (i, 0)),
        out_shape=jax.ShapeDtypeStruct((total, WIDTH + PART + 128), jnp.bfloat16),
        scratch_shapes=[pltpu.VMEM((block + block // 4, WIDTH), jnp.bfloat16)],
        compiler_params=pltpu.CompilerParams(vmem_limit_bytes=62_000_000),
        cost_estimate=pl.CostEstimate(
            flops=16_000_000_000, bytes_accessed=25_000_000, transcendentals=1_000_000
        ),
        name="experts",
    )(rows, back, gate_up)


def combine_body(head_ref, tail_ref, rows_ref, out_ref):
    tokens = out_ref.shape[0]

    def split(value):
        coarse = value.astype(jnp.bfloat16)
        fine = (value - coarse.astype(jnp.float32)).astype(jnp.bfloat16)
        return jnp.concatenate([coarse, fine], axis=0)

    head = split(head_ref[...])
    quarter = quarter_of(tail_ref.shape, 1)

    @pl.loop(0, 4)
    def _(q):
        columns = pl.ds(pl.multiple_of(q * PART, PART), PART)
        weights = split(jnp.where(quarter == q, tail_ref[...], 0.0))
        total = dot(head, rows_ref[:, columns]) + dot(weights, rows_ref[:, WIDTH : WIDTH + PART])
        out_ref[:, columns] = total[:tokens] + total[tokens:]


def combine(head_weights, tail_weights, rows):
    return pl.pallas_call(
        combine_body,
        out_shape=jax.ShapeDtypeStruct((head_weights.shape[0], WIDTH), jnp.float32),
        name="combine",
    )(head_weights, tail_weights, rows)


def shards(
    samples,
    req_frames,
    w_in,
    w_up_aud,
    w_down_aud,
    w_out,
    norm_gain,
    expert_ids,
    gate_weights,
    cotangent,
    w_gate_up,
    w_down,
):
    local_rows = samples[0]
    request_total, slab, hop = local_rows.shape
    grads = cotangent[0]
    tokens, width = grads.shape
    experts = lax.axis_size("section") * lax.axis_size("ep")
    senders = lax.axis_size("ep")
    requests = request_total // senders

    arrived = lax.all_to_all(
        local_rows.reshape(senders, requests * slab, hop),
        "ep",
        split_axis=0,
        concat_axis=0,
        tiled=True,
    ).reshape(-1, hop)

    ids = expert_ids[0].T
    names = ids[:, None, :] == jnp.arange(experts, dtype=jnp.int32)[None, :, None]
    member = jnp.any(names, axis=0)
    before = jnp.asarray(np.triu(np.ones((tokens, tokens)), 1), jnp.bfloat16)
    rank = dot(member.astype(jnp.bfloat16), before).astype(jnp.int32)
    rank = jnp.where(member, rank, -1)
    place = jnp.arange(HEAD, dtype=jnp.int32)[None, :, None]
    head_slots = (rank[:, None, :] == place).reshape(-1, tokens)
    tail_slots = (rank[:, None, :] == HEAD + place % TAIL).reshape(-1, tokens)
    arrived_grads = exchange(pack(rank, grads))

    lengths = req_frames[0, 0]
    ends = jnp.cumsum(lengths)
    places = jnp.arange(tokens, dtype=jnp.int32)
    later = places[:, None] >= ends[None, :-1]
    request = jnp.sum(later.astype(jnp.int32), axis=-1)
    times = places - jnp.sum(jnp.where(later, lengths[None, :-1], 0), axis=-1)
    parts = []
    for offset in range(3):
        at = times + offset
        row = jnp.where(at < TIME, (at // slab) * (requests * slab) + request * slab + at % slab, -1)
        pick = (row[:, None] == jnp.arange(arrived.shape[0], dtype=jnp.int32)).astype(jnp.float32)
        parts.append(jnp.dot(pick, arrived, precision=HIGHEST, preferred_element_type=jnp.float32))
    frames = jnp.concatenate(parts, axis=-1)[:, :NFFT]

    bins_count = NFFT // 2 + 1
    spectrum = jnp.dot(
        frames,
        jnp.asarray(dft_windowed(NFFT, bins_count)),
        precision=HIGHEST,
        preferred_element_type=jnp.float32,
    )
    power = spectrum[:, :256] ** 2 + spectrum[:, 256:] ** 2
    table = np.zeros((256, w_in.shape[0]), np.float32)
    table[:bins_count] = mel_table(bins_count, w_in.shape[0], NFFT)
    energy = jnp.dot(
        power, jnp.asarray(table), precision=HIGHEST, preferred_element_type=jnp.float32
    )
    log_mel = jnp.log(jnp.maximum(energy, MEL_FLOOR)).astype(jnp.bfloat16)
    time_pick = (times[:, None] == jnp.arange(TIME, dtype=jnp.int32)).astype(jnp.float32)
    position = jnp.dot(
        time_pick,
        jnp.asarray(sinusoid_table(TIME, w_in.shape[1])),
        precision=HIGHEST,
        preferred_element_type=jnp.float32,
    )
    state = dot(log_mel, w_in) + position
    normed_audio = layer_norm(state).astype(jnp.bfloat16)

    def half_product(values):
        hidden = jax.nn.gelu(dot(values, w_up_aud), approximate=False).astype(jnp.bfloat16)
        return dot(hidden, w_down_aud)

    other = swap(normed_audio)
    theirs = half_product(other).astype(jnp.bfloat16)
    ours = half_product(normed_audio)
    added = swap(theirs)
    encoded = state + (ours + added.astype(jnp.float32))
    final_audio = layer_norm(encoded).astype(jnp.bfloat16)
    values = dot(final_audio, w_out).astype(jnp.bfloat16).astype(jnp.float32)
    normed = normalize(values, norm_gain).astype(jnp.bfloat16)

    normed, arrived_grads = lax.optimization_barrier((normed, arrived_grads))
    arrived_rows = exchange(pack(rank, normed))
    back = back_run(arrived_grads, w_down[0])
    returned = exchange(experts_run(arrived_rows, back, w_gate_up[0]))

    weight = jnp.sum(jnp.where(names, gate_weights[0].T[:, None, :], 0.0), axis=0)
    weight = jnp.broadcast_to(weight[:, None, :], (experts, HEAD, tokens)).reshape(-1, tokens)
    d_normed = combine(
        jnp.where(head_slots, weight, 0.0).T, jnp.where(tail_slots, weight, 0.0).T, returned
    )
    d_values = jax.vjp(lambda inner: normalize(inner, norm_gain), values)[1](d_normed)[0]
    grad_x = (grads.astype(jnp.float32) + d_values).astype(jnp.bfloat16)

    scalars = returned[:, WIDTH + PART :].astype(jnp.float32)
    first = (jnp.arange(experts * HEAD) % HEAD < TAIL)[:, None]
    picked = jnp.where(head_slots, scalars[:, :1], 0.0)
    picked = picked + jnp.where(tail_slots & first, scalars[:, 64:65], 0.0)
    by_token = jnp.sum(picked.reshape(experts, HEAD, tokens), axis=1)
    grad_w = jnp.sum(jnp.where(names, by_token[None], 0.0), axis=1).T.astype(jnp.bfloat16)
    return (grad_x[None], grad_w[None])


def solution(mesh):
    in_specs = (
        P(("section", "dp"), None, "ep", None),
        P(("section", "dp"), "ep", None),
        P(),
        P(None, "dp"),
        P("dp", None),
        P(),
        P(),
        P(("section", "dp"), "ep", None),
        P(("section", "dp"), "ep", None),
        P(("section", "dp"), "ep", None),
        P(("section", "ep"), None, None),
        P(("section", "ep"), None, None),
    )
    out_specs = (P(("section", "dp"), "ep", None), P(("section", "dp"), "ep", None))
    return jax.shard_map(shards, mesh=mesh, in_specs=in_specs, out_specs=out_specs, check_vma=False)
```
